512 devices in a mesh: wide: 32 (over z_lo, x), narrow: 16 (over z_hi, y, core).
Axes of the slice: x: 4, y: 4, z: 16 (z_hi: 2, z_lo: 8; z = z_hi * 8 + z_lo), core: 2. Of those that a mesh axis runs over, the one named last changes fastest.
Arguments:
- jacobian: bfloat16 [2048, 16384], P(None, ('wide', 'narrow')), may hold values from -0.125 to 0.125
- variance: float32 [2048], replicated, may hold values from 0.1 to 10
Outputs:
- hessian: float32 [16384, 16384], P('wide', 'narrow')
The draws below stay inside these ranges and needn't reach their ends.
All inputs are finite; a program needn't handle non-finite values.
Results may differ from the reference program's by a relative error of at most 0.004.
Values may be sent and summed in bfloat16 or wider, within the bound.
A program may use at most 64 MiB of HBM per device.

```python
import math
import jax
import jax.numpy as jnp
from jax import lax

STATE = 16384
OBS = 2048


def block_scale(own_key, extent, pieces, smallest, largest):
    def one(axis_at, shards_of):
        draws = jax.random.uniform(jax.random.fold_in(jax.random.fold_in(own_key, 6), axis_at), (shards_of,), jnp.float32, smallest / len(pieces), largest / len(pieces))
        return jnp.repeat(jnp.exp(draws), extent[axis_at] // shards_of).reshape((-1,) + (1,) * (len(extent) - axis_at - 1))

    gain = one(*pieces[0])
    for cut in pieces[1:]:
        gain = gain * one(*cut)
    return gain


def centred(stream_key, shape, width, most, shards=(), dtype=jnp.bfloat16):
    result = width * jax.random.normal(stream_key, shape, jnp.float32)
    if shards:
        result = result * block_scale(stream_key, shape, shards, -0.22, 0.18)
    return jnp.clip(result, -most, most).astype(dtype)


def setup_inputs(seed: int = 0) -> dict:
    keys = jax.random.split(jax.random.key(seed), 3)
    jacobian = centred(keys[0], (OBS, STATE), OBS ** -0.5, 0.125, ((1, 512),))
    variance = jnp.clip(jnp.exp(jax.random.uniform(keys[1], (OBS,), jnp.float32, math.log(0.1), math.log(10.0))), 0.1, 10.0)
    return {"jacobian": jacobian, "variance": variance}


def reference(jacobian, variance):
    weights = lax.rsqrt(variance)
    scaled = (jacobian.astype(jnp.float32) * weights[:, None]).astype(jnp.bfloat16)
    return lax.dot_general(scaled, scaled, (((0,), (0,)), ((), ())), preferred_element_type=jnp.float32)
```

```python
import jax
import jax.numpy as jnp
from jax import lax
from jax.experimental import pallas as pl
from jax.experimental.pallas import tpu as pltpu
from jax.sharding import PartitionSpec as P

MESH = pl.DeviceIdType.MESH
XS, ZS, YS, HALVES, CORES = 4, 8, 4, 2, 2
PIECES = 8
LAST = ZS - 1
KAPPA = 2
FAR_LAG = 3
SIB_LAG = 2
GATHER_AT = (10, 12, 14)
STEPS = 8 + 8 + SIB_LAG + 1


def kernel(
    jac_ref, var_ref, out_ref, row, col, acc,
    row_recv, col_recv, send_y, send_e, send_f, send_z, send_x, out_sem,
):
    width = jac_ref.shape[0]
    half = width // 2
    panel = 2 * PIECES * width
    wide, narrow = lax.axis_index("wide"), lax.axis_index("narrow")
    x, zl = lax.rem(wide, XS), lax.div(wide, XS)
    core = lax.rem(narrow, CORES)
    y = lax.rem(lax.div(narrow, CORES), YS)
    zh = lax.div(narrow, CORES * YS)
    odd = lax.rem(x, 2)
    own_plane = zh * YS + y
    primary = lax.div(x, 2) == core
    primary_i = primary.astype(jnp.int32)

    def device(x=x, y=y, zh=zh, zl=zl, core=core):
        return (zl * XS + x, (zh * YS + y) * CORES + core)

    up_y, down_y = lax.rem(y + 1, YS), lax.rem(y + YS - 1, YS)
    far_y = lax.rem(y + 2, YS)
    sibling = device(core=1 - core)
    above, below = device(y=up_y), device(y=down_y)
    opposite = device(zh=1 - zh)
    partner = device(x=x + 1 - 2 * odd)
    other = device(x=lax.rem(x + XS - 1 + 2 * odd, XS))
    near_source = primary & (zl == own_plane)
    far_source = primary & (zl == (1 - zh) * YS + y)
    line_end = primary & (zl == LAST * (1 - zh))
    entry = device(zh=1 - zh, zl=LAST * zh)
    entry_from = device(zh=1 - zh, zl=zh * YS + y)
    z_up, z_down = device(zl=zl + 1), device(zl=zl - 1)
    can_up, can_down = primary & (zl < LAST), primary & (zl > 0)
    k_own = jnp.where(primary, odd, 1 - odd)
    k_other = 1 - k_own

    def piece(h, py, pc):
        return (h * YS + py) * CORES + pc

    def row_at(i, start=0, size=None):
        return row.at[pl.ds(pl.multiple_of(i * width + start, half), size or width)]

    def col_at(k, i):
        return col.at[pl.ds(pl.multiple_of(k * panel + i * width, width), width)]

    def remote(src, dst, send, recv, to):
        return pltpu.make_async_remote_copy(
            src_ref=src, dst_ref=dst, send_sem=send, recv_sem=recv, device_id=to, device_id_type=MESH
        )

    def row_copy(i, send, to, part=0, start=0, size=None):
        ref = row_at(i, start, size)
        return remote(ref, ref, send, row_recv.at[i, part], to)

    def col_copy(k, i, send, to):
        ref = col_at(k, i)
        return remote(ref, ref, send, col_recv.at[k, i], to)

    scale = lax.rsqrt(var_ref[...])
    mine = piece(zh, y, core)
    row_at(mine)[...] = (jac_ref[...].astype(jnp.float32) * scale).astype(jnp.bfloat16)

    barrier = pltpu.get_barrier_semaphore()
    for to in (sibling, above, below, opposite, partner, other):
        pl.semaphore_signal(barrier, inc=1, device_id=to, device_id_type=MESH)
    for present, to in ((can_up, z_up), (can_down, z_down), (far_source, entry), (line_end, entry_from)):

        @pl.when(present)
        def _():
            pl.semaphore_signal(barrier, inc=1, device_id=to, device_id_type=MESH)

    expected = 6 + sum(p.astype(jnp.int32) for p in (can_up, can_down, far_source, line_end))
    pl.semaphore_wait(barrier, expected)

    def y_copies(hi, h):
        own, lo, up, far = (piece(h, v, core) for v in (y, down_y, up_y, far_y))
        sems = [send_y.at[hi, i] for i in range(8)]
        return dict(
            own_up=row_copy(own, sems[0], above),
            own_down=row_copy(own, sems[1], below),
            own_sib=row_copy(own, sems[2], sibling),
            lo_up=row_copy(lo, sems[3], above, 0, 0, half),
            lo_sib=row_copy(lo, sems[4], sibling),
            up_down=row_copy(up, sems[5], below, 1, half, half),
            up_sib=row_copy(up, sems[6], sibling),
            far_sib=row_copy(far, sems[7], sibling),
            far_lo=row_copy(far, sems[7], above, 0, 0, half),
            far_hi=row_copy(far, sems[7], below, 1, half, half),
        )

    near_y, far_rows = y_copies(0, zh), y_copies(1, 1 - zh)

    def gather_own(cp):
        cp["own_up"].start()
        cp["own_down"].start()
        cp["own_sib"].start()

    def gather_up(cp):
        cp["up_sib"].wait_recv()
        cp["up_down"].start()
        cp["up_sib"].start()

    def gather_low(cp):
        cp["lo_sib"].wait_recv()
        cp["lo_up"].start()
        cp["lo_sib"].start()

    def gather_far(cp):
        cp["far_lo"].wait_recv()
        cp["far_hi"].wait_recv()
        cp["far_sib"].start()

    exchange = row_copy(mine, send_e.at[0], opposite)
    exchanged = piece(1 - zh, y, core)

    def order(h, j):
        q = lax.div(j, 2)
        turn = q + lax.div(q, 2) - 2 * lax.div(q, 3)
        return piece(h, lax.rem(y + turn, YS), lax.rem(core + j, CORES))

    def sib_wait(h, py):
        row_copy(piece(h, py, 1 - core), send_y.at[0, 0], sibling).wait_recv()

    def feed(j):
        i = order(zh, jnp.int32(j))

        @pl.when(near_source)
        def _():
            pltpu.make_async_copy(row_at(i), col_at(odd, i), col_recv.at[odd, i]).start()

        @pl.when(far_source)
        def _():
            remote(row_at(i), col_at(odd, i), send_f.at[j], col_recv.at[odd, i], entry).start()

    source = near_source | far_source

    def feed_sib(j, py):
        @pl.when(source)
        def _():
            sib_wait(zh, py)

        feed(j)

    gather_own(near_y)
    exchange.start()
    feed(0)
    feed_sib(1, y)
    gather_up(near_y)
    feed(2)
    gather_low(near_y)
    feed_sib(3, up_y)
    feed(4)
    feed_sib(5, down_y)
    gather_far(near_y)
    feed(6)
    feed_sib(7, far_y)

    hops_near = jnp.maximum(zl - own_plane, own_plane - zl)
    hops_far = jnp.where(zh == 0, LAST - zl, zl)
    at_near, at_far = KAPPA * hops_near, KAPPA * hops_far + FAR_LAG
    first = jnp.minimum(at_near, at_far)
    lag_near = jnp.minimum(at_near - first, PIECES)
    lag_far = jnp.minimum(at_far - first, PIECES)

    z_near_up, z_near_down = can_up & (zl >= own_plane), can_down & (zl <= own_plane)
    z_far_up, z_far_down = can_up & (zh == 1), can_down & (zh == 0)
    types = ((0, zh, lag_near, z_near_up, z_near_down), (1, 1 - zh, lag_far, z_far_up, z_far_down))

    def sends(t, h, j, up, down):
        i = order(h, j)
        slot = t * PIECES + j
        relay_own = primary | (lax.rem(j, 2) == 1)
        return (
            (up, col_copy(k_own, i, send_z.at[0, slot], z_up)),
            (down, col_copy(k_own, i, send_z.at[1, slot], z_down)),
            (primary, col_copy(k_own, i, send_x.at[0, slot], other)),
            (relay_own, col_copy(k_own, i, send_x.at[1, slot], partner)),
        )

    def relays(t, h, j):
        i = order(h, j)
        return primary & (lax.rem(j, 2) == 0), col_copy(k_other, i, send_x.at[2, t * PIECES + j], other)

    def step(s, carry):
        for t, h, lag, up, down in types:
            j = s - lag

            @pl.when((j >= 0) & (j < PIECES))
            def _():
                col_copy(k_own, order(h, j), send_f.at[0], other).wait_recv()
                for present, cp in sends(t, h, j, up, down):
                    pl.when(present)(cp.start)

        for t, h, lag, up, down in types:
            j = s - lag - SIB_LAG

            @pl.when(primary & (j >= 0) & (j < PIECES))
            def _():
                present, cp = relays(t, h, j)
                cp.wait_recv()
                pl.when(present)(cp.start)

        @pl.when(s == GATHER_AT[0] - first)
        def _():
            row_copy(exchanged, send_e.at[0], opposite).wait_recv()
            gather_own(far_rows)

        @pl.when(s == GATHER_AT[1] - first)
        def _():
            gather_up(far_rows)
            gather_low(far_rows)

        @pl.when(s == GATHER_AT[2] - first)
        def _():
            gather_far(far_rows)

        return carry

    lax.fori_loop(0, STEPS, step, 0)

    @pl.when(jnp.logical_not(source))
    def _():
        for py in (y, up_y, down_y, far_y):
            sib_wait(zh, py)

    for py in (y, up_y, down_y, far_y):
        sib_wait(1 - zh, py)

    def late(s, carry):
        @pl.when(jnp.logical_not(primary))
        def _():
            col_copy(k_other, s, send_f.at[0], other).wait_recv()

        return carry

    lax.fori_loop(0, 2 * PIECES, late, 0)

    block = PIECES * width

    def out_copy(b):
        at = pl.ds(pl.multiple_of(b * block, block), block)
        return pltpu.make_async_copy(acc.at[:, at], out_ref.at[:, at], out_sem.at[b])

    def multiply(b, carry):
        at = pl.ds(pl.multiple_of(b * block, block), block)
        acc[:, at] = lax.dot_general(
            row[...], col[at, :], (((1,), (1,)), ((), ())), preferred_element_type=jnp.float32
        )
        out_copy(b).start()
        return carry

    lax.fori_loop(0, 4, multiply, 0)

    for cp in (near_y, far_rows):
        for name in ("own_up", "own_down", "own_sib", "lo_up", "lo_sib", "up_down", "up_sib", "far_sib"):
            cp[name].wait_send()
    exchange.wait_send()

    @pl.when(far_source)
    def _():
        for j in range(PIECES):
            i = order(zh, jnp.int32(j))
            remote(row_at(i), col_at(odd, i), send_f.at[j], col_recv.at[odd, i], entry).wait_send()

    def drain(j, carry):
        for t, h, lag, up, down in types:
            for present, cp in (*sends(t, h, j, up, down), relays(t, h, j)):
                pl.when(present)(cp.wait_send)
        return carry

    lax.fori_loop(0, PIECES, drain, 0)
    for b in range(4):
        out_copy(b).wait()


def body(jacobian, variance):
    depth, width = jacobian.shape
    rows, columns = 2 * PIECES * width, 4 * PIECES * width
    vmem = pl.BlockSpec(memory_space=pltpu.VMEM)
    dma = pltpu.SemaphoreType.DMA
    return pl.pallas_call(
        kernel,
        out_shape=jax.ShapeDtypeStruct((rows, columns), jnp.float32),
        in_specs=[vmem, vmem],
        out_specs=pl.BlockSpec(memory_space=pl.ANY),
        scratch_shapes=[
            pltpu.VMEM((rows, depth), jnp.bfloat16),
            pltpu.VMEM((columns, depth), jnp.bfloat16),
            pltpu.VMEM((rows, columns), jnp.float32),
            dma((16, 2)), dma((2, 16)), dma((2, 8)), dma((1,)), dma((8,)), dma((2, 16)), dma((3, 16)), dma((4,)),
        ],
        compiler_params=pltpu.CompilerParams(collective_id=0, has_side_effects=True),
    )(jacobian.T, variance.reshape(1, depth))


def solution(mesh):
    placed = (P(None, ("wide", "narrow")), P())
    return jax.shard_map(
        body, mesh=mesh, in_specs=placed, out_specs=P("wide", "narrow"), check_vma=False
    )
```
